32 devices in a mesh: seq: 2 (over x), mp: 16 (over z, y, core).
Axes of the slice: x: 2, y: 2, z: 4, core: 2. Of those that a mesh axis runs over, the one named last changes fastest.
Arguments:
- tokens: bfloat16 [512, 4, 1536], P('seq'), may hold values from -6 to 6
- target: bfloat16 [512, 4, 1536], P(('seq', 'mp')), may hold values from -6 to 6
- lengths: int32 [4], replicated, may hold values from 128 to 512, as said below
- routes: int32 [512, 4, 6], P(('seq', 'mp')), may hold values from 0 to 15, all different within a row; in each aligned block of 64 rows (0 to 63, 64 to 127, ..., all dimensions but the last counted through in order) at most 48 rows name the same one
- route_weight: float32 [512, 4, 6], P(('seq', 'mp')), may hold values from 0.1 to 0.4
- in_gain: bfloat16 [1536], P(('seq', 'mp')), may hold values from 0.5 to 1.5
- gate_proj: bfloat16 [1536, 3072], P(None, 'mp'), may hold values from -0.15625 to 0.15625
- value_proj: bfloat16 [1536, 3072], P(None, 'mp'), may hold values from -0.15625 to 0.15625
- state_proj: bfloat16 [1536, 256], P(('seq', 'mp')), may hold values from -0.078125 to 0.078125
- step_proj: bfloat16 [1536, 48], P(None, 'mp'), may hold values from -0.15625 to 0.15625
- conv_value: float32 [4, 3072], P(None, 'mp'), may hold values from -3 to 3
- conv_value_bias: float32 [3072], P('mp'), may hold values from -3 to 3
- conv_state: bfloat16 [256, 4], P(('seq', 'mp')), may hold values from -3 to 3
- conv_state_bias: bfloat16 [256], P(('seq', 'mp')), may hold values from -3 to 3
- step_bias: float32 [48], P('mp'), may hold values from -4 to -1
- decay_log: float32 [48], P('mp'), may hold values from -8 to -1
- skip_gain: float32 [48], P('mp'), may hold values from 0.5 to 2
- mixer_gain: float32 [3072], P('mp'), may hold values from 0.5 to 1.5
- out_proj: bfloat16 [3072, 1536], P('mp'), may hold values from -0.109375 to 0.109375
- ffn_gain: bfloat16 [1536], P(('seq', 'mp')), may hold values from 0.5 to 1.5
- shared_gate: bfloat16 [1536, 1024], P(('seq', 'mp')), may hold values from -0.15625 to 0.15625
- shared_up: bfloat16 [1536, 1024], P(('seq', 'mp')), may hold values from -0.15625 to 0.15625
- shared_down: bfloat16 [1024, 1536], P(('seq', 'mp')), may hold values from -0.1875 to 0.1875
- expert_gate: bfloat16 [16, 1536, 512], P('mp'), may hold values from -0.15625 to 0.15625
- routed_up_weights: bfloat16 [16, 1536, 512], P('mp'), may hold values from -0.15625 to 0.15625
- expert_down: bfloat16 [16, 512, 1536], P('mp'), may hold values from -0.25 to 0.25
Outputs:
- block_out: bfloat16 [512, 4, 1536], P(('seq', 'mp'))
- tokens_grad: float32 [512, 4, 1536], P(('seq', 'mp'))
- in_gain_grad: float32 [1536], P(('seq', 'mp'))
- gate_proj_grad: float32 [1536, 3072], P(None, 'mp')
- value_proj_grad: float32 [1536, 3072], P(None, 'mp')
- state_proj_grad: float32 [1536, 256], P(('seq', 'mp'))
- step_proj_grad: float32 [1536, 48], P(None, 'mp')
- conv_value_grad: float32 [4, 3072], P(None, 'mp')
- conv_value_bias_grad: float32 [3072], P('mp')
- conv_state_grad: float32 [256, 4], P(('seq', 'mp'))
- conv_state_bias_grad: float32 [256], P(('seq', 'mp'))
- step_bias_grad: float32 [48], P('mp')
- decay_log_grad: float32 [48], P('mp')
- skip_gain_grad: float32 [48], P('mp')
- mixer_gain_grad: float32 [3072], P('mp')
- out_proj_grad: float32 [3072, 1536], P('mp')
- ffn_gain_grad: float32 [1536], P(('seq', 'mp'))
- shared_gate_grad: float32 [1536, 1024], P(('seq', 'mp'))
- shared_up_grad: float32 [1536, 1024], P(('seq', 'mp'))
- shared_down_grad: float32 [1024, 1536], P(('seq', 'mp'))
- expert_gate_grad: float32 [16, 1536, 512], P('mp')
- expert_up_grad: float32 [16, 1536, 512], P('mp')
- expert_down_grad: float32 [16, 512, 1536], P('mp')
The draws below stay inside these ranges and needn't reach their ends.
Inputs may be any that keep to these rules, and one draw needn't show every extreme that they name: `routes`: each row names 6 different experts. In each aligned block of 64 rows (the rows of one device), no expert is named by more than 48 rows, a bound that some block reaches. `lengths`: some sequence has all 512 slots true.
All inputs are finite; a program needn't handle non-finite values.
Results may differ from the reference program's by a relative error of at most 0.018.
The reference program's roundings to bfloat16 on the way count: a program that leaves them out, or rounds other values in their place, can miss the bound.
Values may be sent and summed in bfloat16 or wider, within the bound.
No kernel may reach another device: no remote copies, remote signals or barrier semaphores. Data moves between devices by JAX's collectives and lax.ppermute only.
A program may use at most 192 MiB of HBM per device.

```python
import math
import jax
import jax.numpy as jnp
import numpy as np
from jax import lax

D = 1536
HEADS = 48
HEAD_DIM = 64
STATE = 128
CONV = 4
EXPERT_FF = 512
SHARED_FF = 1024
TOPK = 6
NSEQ = 4
SLOT_DEV = 256
INNER = 3072
EXPERTS = 16
SLOTS = 512
ROWS_MP = 64
CAP = 48


def draw_lengths(key, part):
    base_lengths = jax.random.randint(key, (NSEQ,), SLOTS // 4, SLOTS + 1)
    longest = jax.random.randint(jax.random.fold_in(key, 7), (), 0, NSEQ)
    return jnp.where(jnp.arange(NSEQ) == longest, SLOTS, base_lengths).astype(jnp.int32)


def levels(key, extent, cuts, least, largest):
    level, own = 1.0, jax.random.fold_in(key, 6)
    for axis_at, shards_of in cuts:
        steps = jnp.exp(jax.random.uniform(jax.random.fold_in(own, axis_at), (shards_of,), jnp.float32, least / len(cuts), largest / len(cuts)))
        level = level * jnp.repeat(steps, extent[axis_at] // shards_of).reshape([-1 if axis == axis_at else 1 for axis in range(len(extent))])
    return level


def deal_out(stream_key, own, number, rows, count, top, bound, skew):
    sequence = jax.random.permutation(stream_key, count)
    crowded, common = shares(count, rows * top, bound, skew, True), shares(count, rows * top, bound, skew, False)
    places = jnp.arange(count)

    def named(tallies, turn):
        used = int((tallies > 0).sum())
        fixed = max(1, used // 4)
        shifted = fixed + (places - fixed + turn * (used - fixed)) % max(1, count - fixed)
        return jnp.zeros((count,), jnp.int32).at[sequence[jnp.where(places < fixed, places, shifted)]].set(jnp.asarray(tallies, jnp.int32))

    tallies = jnp.where(number % 4 == 0, named(crowded, number // 4), named(common, number - number // 4 - 1))
    mixed = jax.random.permutation(jax.random.fold_in(own, 3), count)
    source_of, taker = mixed[0:count // 2 * 2:2], mixed[1:count // 2 * 2:2]
    margin = jnp.minimum(tallies[source_of] - 1, bound - tallies[taker]) // 2
    margin = jnp.where((source_of == sequence[0]) | (taker == sequence[0]) | (tallies[taker] == 0), 0, jnp.maximum(margin, 0))
    shifted = jax.random.randint(jax.random.fold_in(own, 4), (count // 2,), 0, 1 << 20) % (margin + 1)
    tallies = tallies.at[source_of].add(-shifted).at[taker].add(shifted)
    labels = jnp.searchsorted(jnp.cumsum(tallies), jnp.arange(rows * top), side="right").astype(jnp.int32)
    listing = labels.reshape(top, rows).T
    listing = listing[jax.random.permutation(jax.random.fold_in(own, 1), rows)]
    turn = jax.random.randint(jax.random.fold_in(own, 2), (rows, 1), 0, top)
    return jnp.take_along_axis(listing, (jnp.arange(top)[None, :] + turn) % top, axis=1)


def shares(number_of, total, limit, skew, full):
    loads = [(1 << 20) // math.isqrt(rank ** skew) + 1 for rank in range(1, number_of + 1)]
    largest = limit if full else min(limit, max(-(-total // number_of), total * loads[0] // sum(loads)))
    least = 1 if total - largest >= number_of - 1 else 0
    holding, spare = [largest] + [least] * (number_of - 1), total - largest - least * (number_of - 1)
    while spare > 0:
        free = [i for i in range(1, number_of) if holding[i] < largest] or [i for i in range(1, number_of) if holding[i] < limit]
        pool, budget = sum([loads[i] for i in free]), spare
        for i in free:
            more = min(limit - holding[i], max(1, budget * loads[i] // pool), spare)
            holding[i] = holding[i] + more
            spare = spare - more
    return np.array(holding)


def bell_draw(rng, extent, spread, most, cuts=(), held_as=jnp.bfloat16):
    drawn = jax.random.normal(rng, extent, jnp.float32) * spread
    if len(cuts) > 0:
        drawn = levels(rng, extent, cuts, -0.22, 0.18) * drawn
    return jnp.clip(drawn, min=-most, max=most).astype(held_as)


def setup_inputs(seed: int = 0) -> dict:
    arg_keys = jax.random.split(jax.random.key(seed), 27)
    tokens = bell_draw(arg_keys[0], (SLOTS, NSEQ, D), 1.0, 6.0, ((0, 2),))
    target = bell_draw(arg_keys[1], (SLOTS, NSEQ, D), 1.0, 6.0, ((0, 32),))
    lengths = draw_lengths(jax.random.fold_in(arg_keys[26], 71), 0)
    routes_keys = jax.random.split(jax.random.fold_in(arg_keys[3], 1), SLOTS * NSEQ // ROWS_MP)
    routes_turns = jax.random.permutation(jax.random.fold_in(arg_keys[3], 3), SLOTS * NSEQ // ROWS_MP)
    routes = jax.vmap(lambda own, number: deal_out(jax.random.fold_in(arg_keys[3], 2), own, number, ROWS_MP, EXPERTS, TOPK, CAP, 2))(routes_keys, routes_turns).reshape((SLOTS, NSEQ, TOPK))
    route_weight = jnp.clip(0.1 + 0.3 * jax.random.uniform(arg_keys[4], (SLOTS, NSEQ, TOPK), jnp.float32) ** levels(arg_keys[4], (SLOTS, NSEQ, TOPK), ((0, 32),), -0.2, 0.2), 0.1, 0.4)
    in_gain = jnp.clip(1.0 + 0.1 * jax.random.normal(arg_keys[5], (D,), jnp.float32), 0.5, 1.5).astype(jnp.bfloat16)
    gate_proj = bell_draw(arg_keys[6], (D, INNER), D ** -0.5, 0.15625, ((1, 16),))
    value_proj = bell_draw(arg_keys[7], (D, INNER), D ** -0.5, 0.15625, ((1, 16),))
    state_proj = bell_draw(arg_keys[8], (D, 2 * STATE), (4 * D) ** -0.5, 0.078125, ((0, 32),))
    step_proj = bell_draw(arg_keys[9], (D, HEADS), D ** -0.5, 0.15625, ((1, 16),))
    conv_value = bell_draw(arg_keys[10], (CONV, INNER), 0.5, 3.0, ((1, 16),), jnp.float32)
    conv_value_bias = bell_draw(arg_keys[11], (INNER,), 0.5, 3.0, ((0, 16),), jnp.float32)
    conv_state = bell_draw(arg_keys[12], (2 * STATE, CONV), 0.5, 3.0, ((0, 32),))
    conv_state_bias = bell_draw(arg_keys[13], (2 * STATE,), 0.5, 3.0, ((0, 32),))
    step_bias = jnp.clip(-4.0 + 3.0 * jax.random.uniform(arg_keys[14], (HEADS,), jnp.float32) ** levels(arg_keys[14], (HEADS,), ((0, 16),), -0.2, 0.2), -4.0, -1.0)
    decay_log = jnp.clip(-8.0 + 7.0 * jax.random.uniform(arg_keys[15], (HEADS,), jnp.float32) ** levels(arg_keys[15], (HEADS,), ((0, 16),), -0.2, 0.2), -8.0, -1.0)
    skip_gain = jnp.clip(0.5 + 1.5 * jax.random.uniform(arg_keys[16], (HEADS,), jnp.float32) ** levels(arg_keys[16], (HEADS,), ((0, 16),), -0.2, 0.2), 0.5, 2.0)
    mixer_gain = jnp.clip(1.0 + 0.1 * jax.random.normal(arg_keys[17], (INNER,), jnp.float32), 0.5, 1.5)
    out_proj = bell_draw(arg_keys[18], (INNER, D), INNER ** -0.5, 0.109375, ((0, 16),))
    ffn_gain = jnp.clip(1.0 + 0.1 * jax.random.normal(arg_keys[19], (D,), jnp.float32), 0.5, 1.5).astype(jnp.bfloat16)
    shared_gate = bell_draw(arg_keys[20], (D, SHARED_FF), D ** -0.5, 0.15625, ((0, 32),))
    shared_up = bell_draw(arg_keys[21], (D, SHARED_FF), D ** -0.5, 0.15625, ((0, 32),))
    shared_down = bell_draw(arg_keys[22], (SHARED_FF, D), SHARED_FF ** -0.5, 0.1875, ((0, 32),))
    expert_gate = bell_draw(arg_keys[23], (EXPERTS, D, EXPERT_FF), D ** -0.5, 0.15625, ((0, 16),))
    routed_up_weights = bell_draw(arg_keys[24], (EXPERTS, D, EXPERT_FF), D ** -0.5, 0.15625, ((0, 16),))
    expert_down = bell_draw(arg_keys[25], (EXPERTS, EXPERT_FF, D), EXPERT_FF ** -0.5, 0.25, ((0, 16),))
    return dict(tokens=tokens, target=target, lengths=lengths, routes=routes, route_weight=route_weight, in_gain=in_gain, gate_proj=gate_proj, value_proj=value_proj, state_proj=state_proj, step_proj=step_proj, conv_value=conv_value, conv_value_bias=conv_value_bias, conv_state=conv_state, conv_state_bias=conv_state_bias, step_bias=step_bias, decay_log=decay_log, skip_gain=skip_gain, mixer_gain=mixer_gain, out_proj=out_proj, ffn_gain=ffn_gain, shared_gate=shared_gate, shared_up=shared_up, shared_down=shared_down, expert_gate=expert_gate, routed_up_weights=routed_up_weights, expert_down=expert_down)


epsilon = 1e-05
highest = lax.Precision.HIGHEST

@jax.custom_vjp
def low(v):
    return lax.optimization_barrier(v.astype(jnp.bfloat16)).astype(jnp.float32)

@jax.custom_vjp
def low_back(v):
    return v

def low_keep(v):
    return (low(v), None)

def low_pass(kept, grad):
    return (grad,)

def back_keep(v):
    return (v, None)

def back_low(kept, grad):
    return (low(grad),)
low.defvjp(low_keep, low_pass)
low_back.defvjp(back_keep, back_low)

def project(left_side, matrix):
    return jnp.dot(left_side, matrix, precision=highest, preferred_element_type=jnp.float32)

def rms_scale(values, gain):
    return values * lax.rsqrt(lax.optimization_barrier(jnp.mean(values * values, axis=-1, keepdims=True)) + epsilon) * gain

def conv_decay(extended, conv_weight, conv_bias, step_raw, step_bias, decay_log, inner_width, state_width):
    length = step_raw.shape[0]
    preact = conv_bias + conv_weight[0] * extended[0:length]
    for offset in range(1, conv_weight.shape[0]):
        preact = preact + conv_weight[offset] * extended[offset:offset + length]
    activated = jax.nn.silu(preact)
    head_count = step_raw.shape[-1]
    values = activated[..., :inner_width].reshape(length, activated.shape[1], head_count, inner_width // head_count)
    input_matrix_b = activated[..., inner_width:inner_width + state_width]
    c_matrix = activated[..., inner_width + state_width:]
    step_size = jax.nn.softplus(step_raw + step_bias)
    log_decay = -jnp.exp(decay_log) * step_size
    return (values, input_matrix_b, c_matrix, step_size, log_decay)

def ssd_output(values, input_matrix_b, c_matrix, step_size, log_decay, entering, skip_gain):
    cumulative = jnp.cumsum(log_decay, axis=0)
    length = cumulative.shape[0]
    causal = (jnp.arange(length)[:, None] >= jnp.arange(length)[None, :])[:, :, None, None]
    log_gap = jnp.where(causal, cumulative[:, None] - cumulative[None, :], 0.0)
    decay_mask = jnp.where(causal, jnp.exp(log_gap), 0.0)
    intersection = jnp.einsum('tbn,sbn->tsb', c_matrix, input_matrix_b, precision=highest)
    weighted = decay_mask * intersection[..., None]
    scaled = values * step_size[..., None]
    within = jnp.einsum('tsbh,sbhp->tbhp', weighted, scaled, precision=highest)
    carried = jnp.exp(cumulative)[..., None] * jnp.einsum('tbn,bhpn->tbhp', c_matrix, entering, precision=highest)
    return within + carried + skip_gain[:, None] * values

def state_update(values, input_matrix_b, step_size, log_decay):
    cumulative = jnp.cumsum(log_decay, axis=0)
    decay_total = jnp.exp(cumulative[-1])
    tail_weight = jnp.exp(cumulative[-1] - cumulative) * step_size
    local_state = jnp.einsum('sbh,sbhp,sbn->bhpn', tail_weight, values, input_matrix_b, precision=highest)
    return (decay_total, local_state)

def forward(routes, route_weight, tokens, in_gain, gate_proj, value_proj, state_proj, step_proj, conv_value, conv_value_bias, conv_state, conv_state_bias, step_bias, decay_log, skip_gain, mixer_gain, out_proj, ffn_gain, shared_gate, shared_up, shared_down, expert_gate, routed_up_weights, expert_down):
    normed = low(rms_scale(tokens, in_gain))
    gate_raw = low_back(project(normed, gate_proj))
    value_raw = low_back(project(normed, value_proj))
    state_raw = low_back(project(normed, state_proj))
    step_raw = low_back(project(normed, step_proj))
    conv_input = jnp.concatenate([value_raw, state_raw], axis=-1)
    padding = jnp.zeros((CONV - 1,) + conv_input.shape[1:], jnp.float32)
    extended = jnp.concatenate([padding, conv_input], axis=0)
    conv_weight = jnp.concatenate([conv_value, conv_state.T], axis=1)
    conv_bias = jnp.concatenate([conv_value_bias, conv_state_bias])
    values, input_matrix_b, c_matrix, step_size, log_decay = conv_decay(extended, conv_weight, conv_bias, step_raw, step_bias, decay_log, INNER, STATE)
    block_count = SLOTS // SLOT_DEV

    def blocks(source_array):
        return source_array.reshape((block_count, SLOT_DEV) + source_array.shape[1:])

    def advance(carry_state, pieces):
        block_values, block_b, block_c, block_step, block_decay = pieces
        result = ssd_output(block_values, block_b, block_c, block_step, block_decay, carry_state, skip_gain)
        decay_total, local_state = state_update(block_values, block_b, block_step, block_decay)
        return (decay_total[..., None, None] * carry_state + local_state, result)
    start_state = jnp.zeros((NSEQ, HEADS, HEAD_DIM, STATE), jnp.float32)
    _, outputs = lax.scan(jax.checkpoint(advance), start_state, (blocks(values), blocks(input_matrix_b), blocks(c_matrix), blocks(step_size), blocks(log_decay)))
    mixer_values = outputs.reshape(SLOTS, NSEQ, INNER)
    gated_out = mixer_values * jax.nn.silu(gate_raw)
    square_sum = lax.optimization_barrier(jnp.sum(gated_out * gated_out, axis=-1))
    pre_mix = low_back(project(low(gated_out * mixer_gain), out_proj))
    hidden = tokens + pre_mix * lax.rsqrt(square_sum / INNER + epsilon)[..., None]
    ffn_input = low(rms_scale(hidden, ffn_gain))
    shared_gate_val = low_back(project(ffn_input, shared_gate))
    shared_up_val = low_back(project(ffn_input, shared_up))
    shared_act = low(jax.nn.silu(shared_gate_val) * shared_up_val)
    shared_out = low_back(project(shared_act, shared_down))
    chosen = routes[..., None] == jnp.arange(EXPERTS)
    coefficient = lax.optimization_barrier(jnp.sum(jnp.where(chosen, route_weight[..., None], 0.0), axis=-2))

    def expert_step(running, pieces):
        gate_weight, up_weight, down_weight, share_weight = pieces
        copied = low_back(ffn_input)
        gate_activation = low_back(project(copied, gate_weight))
        up_val = low_back(project(copied, up_weight))
        act_val = low(jax.nn.silu(gate_activation) * up_val)
        result = low_back(low(project(act_val, down_weight)))
        return (running + share_weight[..., None] * result, None)
    routed, _ = lax.scan(jax.checkpoint(expert_step), jnp.zeros_like(tokens), (expert_gate, routed_up_weights, expert_down, jnp.moveaxis(coefficient, -1, 0)))
    return hidden + shared_out + routed

def reference(tokens, target, lengths, routes, route_weight, in_gain, gate_proj, value_proj, state_proj, step_proj, conv_value, conv_value_bias, conv_state, conv_state_bias, step_bias, decay_log, skip_gain, mixer_gain, out_proj, ffn_gain, shared_gate, shared_up, shared_down, expert_gate, routed_up_weights, expert_down):
    params = tuple((member.astype(jnp.float32) for member in (tokens, in_gain, gate_proj, value_proj, state_proj, step_proj, conv_value, conv_value_bias, conv_state, conv_state_bias, step_bias, decay_log, skip_gain, mixer_gain, out_proj, ffn_gain, shared_gate, shared_up, shared_down, expert_gate, routed_up_weights, expert_down)))
    weights_float = route_weight.astype(jnp.float32)

    def run_block(*floats):
        return forward(routes, weights_float, *floats)
    output, pullback = jax.vjp(run_block, *params)
    valid_mask = (jnp.arange(SLOTS)[:, None] < lengths[None, :]).astype(jnp.float32)
    cotangent = (output - target.astype(jnp.float32)) * valid_mask[..., None]
    gradients = pullback(cotangent)
    return (output.astype(jnp.bfloat16), gradients[0], gradients[1], gradients[2], gradients[3], gradients[4], gradients[5], gradients[6], gradients[7], gradients[8], gradients[9], gradients[10], gradients[11], gradients[12], gradients[13], gradients[14], gradients[15], gradients[16], gradients[17], gradients[18], gradients[19], gradients[20], gradients[21])
```

```python
import functools
from types import SimpleNamespace

import jax
import jax.numpy as jnp
from jax import lax
from jax.experimental import pallas as pl
from jax.experimental.pallas import tpu as pltpu
from jax.sharding import PartitionSpec as P

STATE = 128
INNER = 3072


epsilon = 1e-05
highest = lax.Precision.HIGHEST
f32 = jnp.float32
bf16 = jnp.bfloat16


def shifted(block, axis, distance):
    devices = range(lax.axis_size(axis))
    route = [(i - distance, i) for i in devices if i - distance in devices]
    return lax.ppermute(block, axis, route)


def entering_2(value, axis, join, neutral, backward):
    count, mine = (lax.axis_size(axis), lax.axis_index(axis))
    pieces = jax.tree.map(lambda part: lax.all_gather(part, axis), value)
    if backward:
        pieces = jax.tree.map(lambda part: part[::-1], pieces)
        mine = count - 1 - mine
    running = jax.tree.map(
        lambda part, zero: jnp.full_like(part, 0) + jnp.asarray(zero, part.dtype), value, neutral
    )

    def hop(position, running):
        longer = join(running, jax.tree.map(lambda part: part[position], pieces))
        return jax.tree.map(lambda new, old: jnp.where(position < mine, new, old), longer, running)

    return lax.fori_loop(0, count - 1, hop, running)


def rms_scale(values, gain):
    return values * lax.rsqrt(jnp.mean(values * values, axis=-1, keepdims=True) + epsilon) * gain


def silu_slope(values):
    sigmoid_val = jax.nn.sigmoid(values)
    return sigmoid_val * (1.0 + values * (1.0 - sigmoid_val))


def chain_combine(earlier, latter):
    return (earlier[0] * latter[0], latter[0][..., None, None] * earlier[1] + latter[1])


NN = ((1,), (0,))
NT = ((1,), (1,))
TN = ((0,), (0,))
PAD = 8


def mul(a, b, dims, precision=highest):
    return lax.dot_general(a, b, (dims, ((), ())), precision=precision, preferred_element_type=f32)


def iota(shape, axis):
    return lax.broadcasted_iota(jnp.int32, shape, axis)


class Mixer:
    def __init__(self, proj, conv, head, lane, heads, inner):
        self.heads, self.inner, self.dim = heads, inner, inner // heads
        self.iw = lane.shape[1]
        self.ew = self.iw + 2 * STATE
        length = proj.shape[0] - PAD
        self.length, self.window = length, 4
        pre = conv[4:5, :]
        for k in range(self.window):
            pre = pre + conv[k : k + 1, :] * self.tap(proj, k)
        self.pre = pre
        self.sig = jax.nn.sigmoid(pre)
        act = pre * self.sig
        self.v = act[:, : self.iw]
        self.b = act[:, self.iw : self.iw + STATE]
        self.c = act[:, self.iw + STATE :]
        self.raw = proj[PAD:, self.ew + self.iw :] + head[0:1, :]
        self.dt = jnp.maximum(self.raw, 0.0) + jnp.log1p(jnp.exp(-jnp.abs(self.raw)))
        self.rate = -jnp.exp(head[1:2, :])
        self.ld = self.rate * self.dt
        self.mask = iota((length, length), 0) >= iota((length, length), 1)
        self.tri = self.mask.astype(f32)
        self.cum = mul(self.tri, self.ld, NN)
        self.last = self.cum[length - 1 :, :]
        self.gate = proj[PAD:, self.ew : self.ew + self.iw]

    def tap(self, proj, k):
        start = PAD + 1 - self.window + k
        return proj[start : start + self.length, : self.ew]

    def wide(self, x):
        lanes = iota((x.shape[0], self.iw), 1)
        out = jnp.broadcast_to(x[:, self.heads - 1 : self.heads], lanes.shape)
        for h in reversed(range(self.heads - 1)):
            out = jnp.where(lanes < (h + 1) * self.dim, x[:, h : h + 1], out)
        return out

    def narrow(self, x):
        pick = (iota((self.iw, 128), 0) // self.dim == iota((self.iw, 128), 1)).astype(f32)
        return mul(x, pick, NN)

    def of_head(self, x, h):
        return jnp.where(iota(x.shape, 1) // self.dim == h, x, 0.0)

    def decay(self, h, turned):
        gap = self.cum[:, h : h + 1] - turned[h : h + 1, :]
        return jnp.exp(jnp.where(self.mask, gap, -1e30))


def state_kernel(heads, inner, table, proj, conv, head, lane, state_out, total_out):
    m = Mixer(proj, conv, head, lane, heads, inner)
    tail = m.wide(jnp.exp(m.last - m.cum) * m.dt)
    state_out[...] = mul(m.v * tail, m.b, TN)
    total_out[...] = jnp.broadcast_to(jnp.exp(m.last), total_out.shape)


def forward_kernel(heads, inner, table, proj, conv, head, lane, enter, scaled_out, y_out):
    m = Mixer(proj, conv, head, lane, heads, inner)
    scores = mul(m.c, m.b, NT)
    turned = jnp.transpose(m.cum)
    xs = m.v * m.wide(m.dt)
    y = jnp.exp(m.wide(m.cum)) * mul(m.c, enter[...], NT) + lane[0:1, :] * m.v
    for h in range(heads):
        y = y + mul(scores * m.decay(h, turned), m.of_head(xs, h), NN)
    y_out[...] = y
    gated = y * m.gate * jax.nn.sigmoid(m.gate)
    square = jnp.sum(gated * gated, axis=1, keepdims=True)
    high = square.astype(bf16).astype(f32)
    lanes = iota(gated.shape, 1)
    scaled = jnp.where(lanes == inner, high, jnp.where(lanes == inner + 1, square - high, gated * lane[1:2, :]))
    scaled = scaled.astype(bf16)
    count = scaled_out.shape[0]
    size = m.length // count
    for j in range(count):
        scaled_out[table[j]] = scaled[j * size : (j + 1) * size]


def gate_kernel(heads, inner, table, proj, conv, head, lane, y_in, sg_in, enter_grad, dy_out, dgate_out, gain_out, sg):
    m = Mixer(proj, conv, head, lane, heads, inner)
    count = sg_in.shape[0]
    size = m.length // count
    for j in range(count):
        sg[j * size : (j + 1) * size, :] = sg_in[table[j]]
    sum_grad = sg[:, inner : inner + 1] + sg[:, inner + 1 : inner + 2]
    sig = jax.nn.sigmoid(m.gate)
    silu = m.gate * sig
    y = y_in[...]
    gated = y * silu
    grad = sg[...] * lane[1:2, :] + 2.0 * gated * sum_grad
    dy = grad * silu
    dy_out[...] = dy
    dgate_out[...] = (grad * y * sig * (1.0 + m.gate * (1.0 - sig))).astype(bf16)
    gain_out[...] = jnp.broadcast_to(jnp.sum(sg[...] * gated, axis=0, keepdims=True), gain_out.shape)
    enter_grad[...] = mul(jnp.exp(m.wide(m.cum)) * dy, m.c, TN)


def backward_kernel(
    heads, inner, table, proj, conv, head, lane, dy_in, dgate_in, enter_in, exit_in,
    turned_out, plain_out, edge_out, tail_out, sums_out, dpad,
):
    m = Mixer(proj, conv, head, lane, heads, inner)
    length = m.length
    dy, enter, leave = dy_in[...], enter_in[...], exit_in[...]
    scores = mul(m.c, m.b, NT)
    turned = jnp.transpose(m.cum)
    dtw = m.wide(m.dt)
    xs = m.v * dtw
    fade = jnp.exp(m.last - m.cum)
    tail = fade * m.dt
    tailw = m.wide(tail)
    grow = jnp.exp(m.wide(m.cum)) * dy
    dscores = jnp.zeros((length, length), f32)
    dxs = jnp.zeros_like(dy)
    dcum = jnp.zeros((length, 128), f32)
    cols = jnp.zeros((128, length), f32)
    for h in range(heads):
        decay = m.decay(h, turned)
        dyh = m.of_head(dy, h)
        g = mul(dyh, xs, NT)
        weighted = scores * decay
        dscores = dscores + decay * g
        p = weighted * g
        dcum = jnp.where(iota(dcum.shape, 1) == h, jnp.sum(p, axis=1, keepdims=True), dcum)
        cols = jnp.where(iota(cols.shape, 0) == h, jnp.sum(p, axis=0, keepdims=True), cols)
        dxs = dxs + mul(weighted, dyh, TN)
    dcum = dcum - jnp.transpose(cols)
    dc = mul(dscores, m.b, NN) + mul(grow, enter, NN)
    db = mul(dscores, m.c, TN) + mul(tailw * m.v, leave, NN)
    u = mul(m.b, leave, NT)
    dtail = m.narrow(m.v * u)
    dcum = dcum + m.narrow(grow * mul(m.c, enter, NT)) - dtail * tail
    pick = (iota((m.iw, 128), 0) // m.dim == iota((m.iw, 128), 1)).astype(f32)
    total = jnp.sum(mul(enter * leave, pick, TN), axis=0, keepdims=True)
    dlast = jnp.sum(dtail * tail, axis=0, keepdims=True) + total * jnp.exp(m.last)
    dcum = dcum + jnp.where(iota(dcum.shape, 0) == length - 1, dlast, 0.0)
    dld = mul(m.tri, dcum, TN)
    ddt = dtail * fade + m.narrow(dxs * m.v) + m.rate * dld
    dstep = ddt * jax.nn.sigmoid(m.raw)
    dstep = jnp.where(iota(dstep.shape, 1) < heads, dstep, 0.0)
    dv = dxs * dtw + lane[0:1, :] * dy + tailw * u
    dpre = jnp.concatenate([dv, db, dc], axis=1) * (m.sig * (1.0 + m.pre * (1.0 - m.sig)))
    dpad[0:PAD, :] = jnp.zeros((PAD, m.ew), f32)
    dpad[PAD : PAD + length, :] = dpre
    dpad[PAD + length :, :] = jnp.zeros((PAD, m.ew), f32)
    dext = jnp.zeros((length + PAD, m.ew), f32)
    sums_out[...] = jnp.zeros(sums_out.shape, f32)
    for k in range(m.window):
        start = m.window - 1 - k
        dext = dext + conv[k : k + 1, :] * dpad[start : start + length + PAD, :]
        sums_out[k : k + 1, :] = jnp.sum(dpre * m.tap(proj, k), axis=0, keepdims=True)
    sums_out[4:5, :] = jnp.sum(dpre, axis=0, keepdims=True)
    sums_out[5:6, : m.iw] = jnp.sum(dy * m.v, axis=0, keepdims=True)
    sums_out[6:7, :128] = jnp.sum(dstep, axis=0, keepdims=True)
    sums_out[7:8, :128] = jnp.sum(m.ld * dld, axis=0, keepdims=True)
    edge_out[...] = dext[:PAD]
    tail_out[...] = dext[length:]
    low = jnp.concatenate([dext[PAD:].astype(bf16), dgate_in[...], dstep.astype(bf16)], axis=1)
    plain_out[0:PAD, :] = jnp.zeros((PAD, low.shape[1]), bf16)
    plain_out[PAD:, :] = low
    count = turned_out.shape[0]
    size = length // count
    for j in range(count):
        turned_out[table[j]] = low[j * size : (j + 1) * size]


def run_mixer(kernel, heads, inner, table, args, outs, scratch=()):
    count = args[0].shape[0]

    def spec(shape):
        if len(shape) == 2:
            return pl.BlockSpec(shape, lambda b, t: (0, 0))
        if len(shape) == 3:
            return pl.BlockSpec((None,) + shape[1:], lambda b, t: (b, 0, 0))
        return pl.BlockSpec((shape[0], None) + shape[2:], lambda b, t: (0, b, 0, 0))

    return pl.pallas_call(
        functools.partial(kernel, heads, inner),
        grid_spec=pltpu.PrefetchScalarGridSpec(
            num_scalar_prefetch=1,
            grid=(count,),
            in_specs=[spec(a.shape) for a in args],
            out_specs=[spec(o.shape) for o in outs],
            scratch_shapes=list(scratch),
        ),
        out_shape=list(outs),
        name=kernel.__name__,
    )(table, *args)


def swap(block, axis, bit):
    count = lax.axis_size(axis)
    return lax.ppermute(block, axis, [(i, i ^ bit) for i in range(count)])


def bits_of(axis):
    count = lax.axis_size(axis)
    bits = []
    while count > 1:
        count //= 2
        bits.append(count)
    return bits


def positions(order):
    places = [0]
    for bit in order:
        places = places + [place | bit for place in places]
    return places


def spread(block, axis, order):
    held = block[None]
    for bit in order:
        held = jnp.concatenate([held, swap(held, axis, bit)], axis=0)
    return held


def collect(blocks, axis, order, sent=bf16, split=None):
    for bit in reversed(order):
        half = blocks.shape[0] // 2
        going = blocks[half:]
        if split is not None:
            value = going[..., split : split + 1] + going[..., split + 1 : split + 2]
            high = lax.reduce_precision(value, 8, 7)
            column = iota(going.shape, going.ndim - 1)
            going = jnp.where(column == split, high, jnp.where(column == split + 1, value - high, going))
        arrived = swap(going.astype(sent), axis, bit)
        blocks = blocks[:half] + arrived.astype(f32)
    return blocks[0]


def trade(blocks, axis, order):
    count = blocks.shape[0]
    rest = blocks.shape[1:]
    view = blocks.reshape((2,) * len(order) + rest)
    for at, bit in enumerate(order):
        axis_at = len(order) - 1 - at
        kept = lax.index_in_dim(view, 0, axis_at)
        sent = lax.index_in_dim(view, 1, axis_at)
        view = jnp.concatenate([kept, swap(sent, axis, bit)], axis=axis_at)
    return view.reshape((count,) + rest)


def reorder(blocks, axis, order):
    return jnp.take(blocks, lax.axis_index(axis) ^ jnp.array(positions(order), jnp.int32), axis=0)


def absolute(blocks, axis, order):
    places = positions(order)
    inverse = [0] * len(places)
    for at, place in enumerate(places):
        inverse[place] = at
    pick = jnp.array(inverse, jnp.int32)[lax.axis_index(axis) ^ jnp.arange(len(places))]
    return jnp.take(blocks, pick, axis=0)


def spread_all(block):
    seq_bits, mp_bits = bits_of("seq"), bits_of("mp")
    held = absolute(spread(block, "seq", seq_bits), "seq", seq_bits)
    held = absolute(spread(held, "mp", mp_bits), "mp", mp_bits)
    held = jnp.moveaxis(held, 1, 0)
    return held.reshape((-1,) + block.shape)


def collect_all(blocks):
    seq_bits, mp_bits = bits_of("seq"), bits_of("mp")
    rest = blocks.shape[1:]
    view = blocks.reshape((lax.axis_size("seq"), lax.axis_size("mp")) + rest)
    mine = collect(reorder(view, "seq", seq_bits), "seq", seq_bits, f32)
    return collect(reorder(mine, "mp", mp_bits), "mp", mp_bits, f32)


def exchange(value):
    for bit in bits_of("seq"):
        low = value.astype(bf16)
        value = low.astype(f32) + swap(low, "seq", bit).astype(f32)
    return value


def exchange_wide(value):
    for bit in bits_of("seq"):
        value = value + swap(value, "seq", bit)
    return value


def body(
    tokens,
    target,
    lengths,
    routes,
    route_weight,
    in_gain,
    gate_proj,
    value_proj,
    state_proj,
    step_proj,
    conv_value,
    conv_value_bias,
    conv_state,
    conv_state_bias,
    step_bias,
    decay_log,
    skip_gain,
    mixer_gain,
    out_proj,
    ffn_gain,
    shared_gate,
    shared_up,
    shared_down,
    expert_gate,
    routed_up_weights,
    expert_down,
):
    seq_devices, mp_devices = lax.axis_size("seq"), lax.axis_size("mp")
    devices = seq_devices * mp_devices
    me = lax.axis_index("mp")
    slots, sequences, width = tokens.shape
    own = slots // mp_devices
    inner = gate_proj.shape[1]
    heads = step_proj.shape[1]
    window = conv_value.shape[0]
    units = expert_gate.shape[2]
    iw = -(-inner // 128) * 128
    ew = iw + 2 * STATE
    chunks = 2
    per = sequences // chunks
    rows = own * per
    bits, seq_bits = bits_of("mp"), bits_of("seq")
    orders = [bits, bits[2:3] + bits[0:2] + bits[3:]] if len(bits) == 4 else [bits, bits]
    tables = []
    for order in orders:
        places = positions(order)
        inverse = [places.index(at) for at in range(mp_devices)]
        tables.append(jnp.array(inverse, jnp.int32)[me ^ jnp.arange(mp_devices)].astype(jnp.int32))

    edge_tokens = shifted(tokens[slots - window + 1 :], "seq", 1)
    x_seq = jnp.concatenate([jnp.zeros((PAD + 1 - window,) + tokens.shape[1:], bf16), edge_tokens, tokens], axis=0)
    x_seq = jnp.transpose(x_seq, (1, 0, 2))
    d_rows = in_gain.shape[0]
    c_rows = conv_state_bias.shape[0]
    small = jnp.concatenate([in_gain, ffn_gain, conv_state.reshape(-1), conv_state_bias])
    small = jnp.pad(small, (0, -small.shape[0] % 128))
    small_all = spread_all(small)
    in_gain_all = small_all[:, :d_rows].reshape(width).astype(f32)
    ffn_gain_all = small_all[:, d_rows : 2 * d_rows].reshape(width).astype(f32)
    at = 2 * d_rows + window * c_rows
    conv_state_all = small_all[:, 2 * d_rows : at].reshape(2 * STATE, window).astype(f32)
    conv_bias_all = small_all[:, at : at + c_rows].reshape(2 * STATE).astype(f32)
    state_all = spread_all(state_proj).reshape(width, 2 * STATE)
    w_all = jnp.concatenate(
        [
            jnp.pad(value_proj, ((0, 0), (0, iw - inner))),
            state_all,
            jnp.pad(gate_proj, ((0, 0), (0, iw - inner))),
            jnp.pad(step_proj, ((0, 0), (0, 128 - heads))),
        ],
        axis=1,
    )
    conv_all = jnp.concatenate(
        [
            jnp.pad(jnp.concatenate([conv_value, conv_value_bias[None]]), ((0, 7 - window), (0, iw - inner))),
            jnp.pad(jnp.concatenate([conv_state_all.T, conv_bias_all[None]]), ((0, 7 - window), (0, 0))),
        ],
        axis=1,
    )
    head_all = jnp.pad(jnp.stack([step_bias, decay_log]), ((0, 6), (0, 128 - heads)))
    lane_all = jnp.pad(jnp.stack([jnp.repeat(skip_gain, inner // heads), mixer_gain]), ((0, 6), (0, iw - inner)))
    out_all = jnp.pad(out_proj, ((0, iw - inner), (0, 128)))
    r, c = iota(out_all.shape, 0), iota(out_all.shape, 1)
    out_all = jnp.where((c >= width) & (c < width + 2) & (r - inner == c - width), 1.0, out_all).astype(bf16)

    ipd = shared_down.shape[0]
    extra = ipd * seq_devices
    pair = jnp.stack([shared_gate, shared_up], 0).reshape(2, d_rows, seq_devices, mp_devices, ipd)
    pair = jnp.transpose(pair, (3, 1, 0, 2, 4)).reshape(mp_devices, d_rows, 2 * extra)
    pair = absolute(trade(reorder(pair, "mp", bits), "mp", bits), "mp", bits)
    pair = absolute(spread(pair, "seq", seq_bits), "seq", seq_bits).reshape(width, 2 * extra)
    down_slice = absolute(spread(shared_down, "seq", seq_bits), "seq", seq_bits).reshape(extra, width)
    w_gate = jnp.concatenate([expert_gate[0], pair[:, :extra]], axis=1)
    w_up = jnp.concatenate([routed_up_weights[0], pair[:, extra:]], axis=1)
    w_down = jnp.concatenate([expert_down[0], down_slice], axis=0)

    named = routes[..., None] == jnp.arange(mp_devices, dtype=jnp.int32)
    coefficient = jnp.sum(jnp.where(named, route_weight[..., None], 0.0), axis=2)
    coefficient = jnp.transpose(coefficient, (1, 0, 2)).reshape(chunks, rows, mp_devices)
    row_coef = []
    for g in range(chunks):
        every = spread(coefficient[g], "mp", orders[g]).reshape(mp_devices * rows, mp_devices)
        mine = jnp.sum(jnp.where(jnp.arange(mp_devices) == me, every, 0.0), axis=1)
        row_coef.append(jnp.where(jnp.arange(units + extra)[None, :] < units, mine[:, None], 1.0))

    targets = jnp.transpose(target, (1, 0, 2)).astype(f32).reshape(chunks, rows, width)
    position = lax.axis_index("seq") * slots + me * own + jnp.arange(own, dtype=jnp.int32)
    valid = (position[None, :] < lengths[:, None]).astype(f32).reshape(chunks, rows, 1)

    def struct(shape, kind=f32):
        return jax.ShapeDtypeStruct(shape, kind)

    def passing(total, state, backward):
        if seq_devices == 2:
            return shifted(state, "seq", -1 if backward else 1)
        split = state[:, :inner].reshape(per, heads, inner // heads, STATE)
        decay = total[:, 0, :heads]
        got = entering_2((decay, split), "seq", chain_combine, (jnp.ones_like(decay), jnp.zeros_like(split)), backward)
        return jnp.pad(got[1].reshape(per, inner, STATE), ((0, 0), (0, iw - inner), (0, 0)))

    kept = [SimpleNamespace() for _ in range(chunks)]
    for g, k in enumerate(kept):
        x = x_seq[g * per : (g + 1) * per]
        k.normed = rms_scale(x.astype(f32), in_gain_all).astype(bf16).reshape(per * (slots + PAD), width)
        proj = mul(k.normed, w_all, NN, None).reshape(per, slots + PAD, w_all.shape[1])
        k.shared = (proj, conv_all, head_all, lane_all)
        state, k.total = run_mixer(
            state_kernel, heads, inner, tables[g], k.shared, [struct((per, iw, STATE)), struct((per, 8, 128))]
        )
        k.entering = passing(k.total, state, False)
    for g, k in enumerate(kept):
        k.scaled, k.y = run_mixer(
            forward_kernel,
            heads,
            inner,
            tables[g],
            k.shared + (k.entering,),
            [struct((mp_devices, per, own, iw), bf16), struct((per, slots, iw))],
        )
        k.scaled = k.scaled.reshape(mp_devices * rows, iw)
        part = mul(k.scaled, out_all, NN, None).reshape(mp_devices, rows, -1)
        mixed = collect(part, "mp", orders[g], split=width)
        k.pre_mix = mixed[:, :width]
        k.inv_norm = lax.rsqrt((mixed[:, width : width + 1] + mixed[:, width + 1 : width + 2]) / INNER + epsilon)
        k.own = lax.dynamic_slice(x_seq, (g * per, PAD + me * own, 0), (per, own, width)).astype(f32).reshape(rows, width)
        k.hidden = k.own + k.pre_mix * k.inv_norm
        ffn_own = rms_scale(k.hidden, ffn_gain_all).astype(bf16)
        k.ffn = spread(ffn_own, "mp", orders[g]).reshape(mp_devices * rows, width)
    for g, k in enumerate(kept):
        k.g = mul(k.ffn, w_gate, NN, None)
        k.u = mul(k.ffn, w_up, NN, None)
        k.act = (row_coef[g] * jax.nn.silu(k.g) * k.u).astype(bf16)
        part = mul(k.act, w_down, NN, None).reshape(mp_devices, rows, width)
        output = k.hidden + collect(part, "mp", orders[g])
        k.out = output.astype(bf16)
        k.grad_out = (output - targets[g]) * valid[g]
        k.grad_low = spread(k.grad_out.astype(bf16), "mp", orders[g]).reshape(mp_devices * rows, width)
    for g, k in enumerate(kept):
        back = mul(k.grad_low, w_down, NT, None) * row_coef[g]
        k.dg = (back * k.u * silu_slope(k.g)).astype(bf16)
        k.du = (back * jax.nn.silu(k.g)).astype(bf16)
        part = mul(k.dg, w_gate, NT, None) + mul(k.du, w_up, NT, None)
        ffn_grad = collect(part.reshape(mp_devices, rows, width), "mp", orders[g])
        _, norm_back = jax.vjp(rms_scale, k.hidden, ffn_gain_all)
        hidden_part, k.ffn_gain_grad = norm_back(ffn_grad)
        k.hidden_grad = k.grad_out + hidden_part
        sum_share = (
            jnp.sum(k.hidden_grad * k.pre_mix, axis=-1, keepdims=True)
            * (-0.5 / INNER) * k.inv_norm * k.inv_norm * k.inv_norm
        )
        high = lax.reduce_precision(sum_share, 8, 7)
        lane = jnp.arange(128)
        more = jnp.where(lane == 0, high, jnp.where(lane == 1, sum_share - high, 0.0))
        packed = jnp.concatenate([k.hidden_grad * k.inv_norm, more], axis=-1).astype(bf16)
        k.mix = spread(packed, "mp", orders[g]).reshape(mp_devices * rows, width + 128)
    for g, k in enumerate(kept):
        scaled_grad = mul(k.mix, out_all, NT, None).reshape(mp_devices, per, own, iw)
        k.enter_grad, k.dy, k.dgate, k.gain_sum = run_mixer(
            gate_kernel,
            heads,
            inner,
            tables[g],
            k.shared + (k.y, scaled_grad),
            [struct((per, iw, STATE)), struct((per, slots, iw)), struct((per, slots, iw), bf16), struct((per, 8, iw))],
            [pltpu.VMEM((slots, iw), f32)],
        )
        k.leaving = passing(k.total, k.enter_grad, True)

    def both(a, b):
        return mul(jnp.concatenate(a, 0), jnp.concatenate(b, 0), TN, None)

    d_down = both([k.act for k in kept], [k.grad_low for k in kept])
    d_gate = both([k.ffn for k in kept], [k.dg for k in kept])
    d_up = both([k.ffn for k in kept], [k.du for k in kept])
    expert_gate_grad = exchange(d_gate[:, :units])[None]
    expert_up_grad = exchange(d_up[:, :units])[None]
    expert_down_grad = exchange(d_down[:units])[None]
    d_pair = jnp.concatenate([d_gate[:, units:], d_up[:, units:]], axis=1)
    d_pair = d_pair.reshape(seq_devices, mp_devices, d_rows, 2 * extra)
    d_pair = collect(reorder(d_pair, "seq", seq_bits), "seq", seq_bits)
    d_pair = reorder(d_pair.astype(bf16), "mp", bits)
    d_pair = absolute(trade(d_pair, "mp", bits), "mp", bits).astype(f32)
    d_pair = d_pair.reshape(mp_devices, d_rows, 2, seq_devices, ipd)
    d_pair = jnp.transpose(d_pair, (2, 1, 3, 0, 4)).reshape(2, d_rows, devices * ipd)
    d_down_own = d_down[units:].reshape(seq_devices, ipd, width)
    shared_down_grad = collect(reorder(d_down_own, "seq", seq_bits), "seq", seq_bits)

    for g, k in enumerate(kept):
        columns = w_all.shape[1]
        turned, plain, edge, tail, k.sums = run_mixer(
            backward_kernel,
            heads,
            inner,
            tables[g],
            k.shared + (k.dy, k.dgate, k.entering, k.leaving),
            [
                struct((mp_devices, per, own, columns), bf16),
                struct((per, slots + PAD, columns), bf16),
                struct((per, PAD, ew)),
                struct((per, PAD, ew)),
                struct((per, 8, ew)),
            ],
            [pltpu.VMEM((slots + 2 * PAD, ew), f32)],
        )
        end = (tail + shifted(edge, "seq", -1)).astype(bf16)
        k.plain = lax.dynamic_update_slice(plain, end, (0, slots, 0)).reshape(per * (slots + PAD), columns)
        turned = lax.dynamic_update_slice(turned, end[None], (tables[g][mp_devices - 1], 0, own - PAD, 0))
        part = mul(turned.reshape(mp_devices * rows, columns), w_all, NT, None)
        normed_grad = collect(part.reshape(mp_devices, rows, width), "mp", orders[g])
        _, first_norm_back = jax.vjp(lambda v: rms_scale(v, in_gain_all), k.own)
        k.tokens_grad = first_norm_back(normed_grad)[0] + k.hidden_grad

    def whole(pieces):
        return jnp.transpose(jnp.concatenate(pieces, 0).reshape(sequences, own, width), (1, 0, 2))

    block_out = whole([k.out for k in kept])
    tokens_grad = whole([k.tokens_grad for k in kept])
    d_out = both([k.scaled for k in kept], [k.mix for k in kept])[:inner, :width]
    d_all = both([k.normed for k in kept], [k.plain for k in kept])
    in_gain_part = jnp.sum(d_all * w_all.astype(f32), axis=1) / in_gain_all
    sums = sum(jnp.sum(k.sums, axis=0) for k in kept)
    gain_sum = sum(jnp.sum(k.gain_sum, axis=0) for k in kept)
    ffn_gain_part = sum(k.ffn_gain_grad for k in kept)
    out_proj_grad = exchange(d_out)
    gate_at = ew + iw
    head_grads = exchange(
        jnp.concatenate([d_all[:, ew : ew + inner], d_all[:, :inner], d_all[:, gate_at : gate_at + heads]], axis=1)
    )
    packed = jnp.concatenate(
        [
            d_all[:, iw:ew].reshape(devices, d_rows * 2 * STATE),
            in_gain_part.reshape(devices, d_rows),
            ffn_gain_part.reshape(devices, d_rows),
            sums[:window, iw:].T.reshape(devices, c_rows * window),
            sums[window, iw:].reshape(devices, c_rows),
        ],
        axis=1,
    )
    packed = jnp.pad(packed, ((0, 0), (0, -packed.shape[1] % 1024))).reshape(devices, -1, 128)
    mine = collect_all(packed).reshape(-1)
    parts, at = [], 0
    for size in (d_rows * 2 * STATE, d_rows, d_rows, c_rows * window, c_rows):
        parts.append(mine[at : at + size])
        at += size
    skips = jnp.sum(sums[5, :inner].reshape(heads, -1), axis=1)
    tiny = jnp.concatenate(
        [sums[: window + 1, :inner].reshape(-1), gain_sum[0, :inner], sums[6, :heads], sums[7, :heads], skips]
    )
    tiny = exchange_wide(tiny)
    at = window * inner
    ends = at + 2 * inner
    return (
        block_out,
        tokens_grad,
        parts[1],
        head_grads[:, :inner],
        head_grads[:, inner : 2 * inner],
        parts[0].reshape(d_rows, 2 * STATE),
        head_grads[:, 2 * inner :],
        tiny[:at].reshape(window, inner),
        tiny[at : at + inner],
        parts[3].reshape(c_rows, window),
        parts[4],
        tiny[ends : ends + heads],
        tiny[ends + heads : ends + 2 * heads],
        tiny[ends + 2 * heads :],
        tiny[at + inner : ends],
        out_proj_grad,
        parts[2],
        d_pair[0],
        d_pair[1],
        shared_down_grad,
        expert_gate_grad,
        expert_up_grad,
        expert_down_grad,
    )


def solution(mesh):
    placed = (
        P("seq", None, None),
        P(("seq", "mp"), None, None),
        P(),
        P(("seq", "mp"), None, None),
        P(("seq", "mp"), None, None),
        P(("seq", "mp")),
        P(None, "mp"),
        P(None, "mp"),
        P(("seq", "mp"), None),
        P(None, "mp"),
        P(None, "mp"),
        P("mp"),
        P(("seq", "mp"), None),
        P(("seq", "mp")),
        P("mp"),
        P("mp"),
        P("mp"),
        P("mp"),
        P("mp", None),
        P(("seq", "mp")),
        P(("seq", "mp"), None),
        P(("seq", "mp"), None),
        P(("seq", "mp"), None),
        P("mp", None, None),
        P("mp", None, None),
        P("mp", None, None),
    )
    return jax.shard_map(
        body,
        mesh=mesh,
        in_specs=placed,
        out_specs=(
            P(("seq", "mp"), None, None),
            P(("seq", "mp"), None, None),
            P(("seq", "mp")),
            P(None, "mp"),
            P(None, "mp"),
            P(("seq", "mp"), None),
            P(None, "mp"),
            P(None, "mp"),
            P("mp"),
            P(("seq", "mp"), None),
            P(("seq", "mp")),
            P("mp"),
            P("mp"),
            P("mp"),
            P("mp"),
            P("mp", None),
            P(("seq", "mp")),
            P(("seq", "mp"), None),
            P(("seq", "mp"), None),
            P(("seq", "mp"), None),
            P("mp", None, None),
            P("mp", None, None),
            P("mp", None, None),
        ),
        check_vma=False,
    )
```
